32 devices in a mesh: grp: 2 (over y), seq: 16 (over z, x, core).
Axes of the slice: x: 2, y: 2, z: 4, core: 2. Of those that a mesh axis runs over, the one named last changes fastest.
Arguments:
- query: bfloat16 [2, 16, 1024, 128], P('grp', None, 'seq'), parts along dimension 0, may hold values from -49 to 49
- key: bfloat16 [2, 16, 1024, 128], P('grp', None, 'seq'), parts along dimension 0, may hold values from -8 to 8
- value: bfloat16 [2, 16, 1024, 128], P('grp', None, 'seq'), parts along dimension 0, may hold values from -6 to 6
- mem_key: bfloat16 [2, 16, 1024, 128], P('grp', None, 'seq'), parts along dimension 0, may hold values from -8 to 8
- mem_value: bfloat16 [2, 16, 1024, 128], P('grp', None, 'seq'), parts along dimension 0, may hold values from -6 to 6
- mem_count: int32 [2, 4], P('grp'), parts along dimension 0, may hold values from 1 to 256, as said below
- mem_factor: int32 [2, 4], P('grp'), parts along dimension 0, may hold values from 1 to 16, as said below
- out_weight: bfloat16 [2048, 3072], P('seq'), may hold values from -0.125 to 0.125
Outputs:
- block_out: bfloat16 [2, 1024, 3072], P('grp', 'seq'), parts along dimension 0
The draws below stay inside these ranges and needn't reach their ends.
There are 2 independent parts, one for each index of `grp`. The reference program is written for one: setup_inputs(seed, part) draws one part's arguments, and reference() takes and returns one part's arrays. A program takes and returns all parts, laid end to end along the dimension named above; an argument that names none is the same for every part. Nothing has to cross between parts.
Inputs may be any that keep to these rules, and one draw needn't show every extreme that they name: `mem_count`: some stretch of every sequence holds exactly 256 live tokens. `mem_factor`: powers of two.
All inputs are finite; a program needn't handle non-finite values.
Results may differ from the reference program's by a relative error of at most 0.0052.
Values may be sent and summed in bfloat16 or wider, within the bound.
A program may use at most 128 MiB of HBM per device.

```python
import jax
import jax.numpy as jnp
from jax import lax

D = 3072
HD = 128
HEADS = 16
STRETCHES = 4
MCAP = 256
SEQS = 1
LEN = 1024
MEM = 1024


def drawn_pair(key):
    base = jax.random.fold_in(key, 7)
    first, second = jax.random.split(base, 2)
    shape = (SEQS, HEADS, LEN, HD)
    keys = jnp.clip(1.6 * jax.random.normal(first, shape, jnp.float32), -8.0, 8.0)
    queries = jnp.clip(1.6 * jax.random.normal(second, shape, jnp.float32), -8.0, 8.0)
    return (jnp.clip(queries, -49.0, 49.0), keys)


def draw_query(key, part):
    return drawn_pair(key)[0].astype(jnp.bfloat16)


def draw_key(key, part):
    return drawn_pair(key)[1].astype(jnp.bfloat16)


def draw_mem_count(key, part):
    first, second = jax.random.split(jax.random.fold_in(key, 11))
    counts = jax.random.randint(first, (SEQS, STRETCHES), 1, MCAP + 1)
    full_stretch = jax.random.randint(second, (SEQS,), 0, STRETCHES)
    counts = counts.at[jnp.arange(SEQS), full_stretch].set(MCAP)
    return counts.astype(jnp.int32)


def draw_mem_factor(key, part):
    first, second = jax.random.split(jax.random.fold_in(key, 13))
    powers = jax.random.randint(first, (SEQS, STRETCHES), 0, 5)
    widest = jax.random.randint(second, (), 0, STRETCHES)
    powers = powers.at[0, widest].set(4)
    return jnp.left_shift(jnp.ones_like(powers), powers).astype(jnp.int32)


def level_of(rng, extent, cuts, smallest, largest):
    level = 1.0
    for dim, blocks in cuts:
        draws = jax.random.uniform(jax.random.fold_in(jax.random.fold_in(rng, 6), dim), (blocks,), jnp.float32, smallest / len(cuts), largest / len(cuts))
        level = level * jnp.repeat(jnp.exp(draws), extent[dim] // blocks).reshape((-1,) + (1,) * (len(extent) - 1 - dim))
    return level


def noise(key, extent, scale, most, cuts=(), dtype=jnp.bfloat16):
    result = scale * jax.random.normal(key, extent, jnp.float32)
    if cuts:
        result = result * level_of(key, extent, cuts, -0.22, 0.18)
    return jnp.clip(result, -most, most).astype(dtype)


def setup_inputs(seed: int = 0, part: int = 0) -> dict:
    key_list = jax.random.split(jax.random.key(seed), 9)
    part_splits = jax.random.split(jax.random.fold_in(key_list[8], part), 9)
    return {
        "query": draw_query(jax.random.fold_in(jax.random.fold_in(key_list[8], part), 71), part),
        "key": draw_key(jax.random.fold_in(jax.random.fold_in(key_list[8], part), 71), part),
        "value": noise(part_splits[2], (SEQS, HEADS, LEN, HD), 1.0, 6.0, ((2, 16),)),
        "mem_key": noise(part_splits[3], (SEQS, HEADS, MEM, HD), 1.6, 8.0, ((2, 16),)),
        "mem_value": noise(part_splits[4], (SEQS, HEADS, MEM, HD), 1.0, 6.0, ((2, 16),)),
        "mem_count": draw_mem_count(jax.random.fold_in(jax.random.fold_in(key_list[8], part), 71), part),
        "mem_factor": draw_mem_factor(jax.random.fold_in(jax.random.fold_in(key_list[8], part), 71), part),
        "out_weight": noise(key_list[7], (HEADS * HD, D), (HEADS * HD) ** -0.5, 0.125, ((0, 16),)),
    }


def reference(query, key, value, mem_key, mem_value, mem_count, mem_factor, out_weight):
    slot = jnp.arange(MEM).astype(jnp.int32)
    stretch_of = slot // MCAP
    offset = slot % MCAP
    scale = HD ** -0.5

    def one_group(index):
        seq_index = index // HEADS
        head_index = index % HEADS
        all_keys = jnp.concatenate([key[seq_index, head_index], mem_key[seq_index, head_index]], 0)
        all_vals = jnp.concatenate([value[seq_index, head_index], mem_value[seq_index, head_index]], 0)
        counts = mem_count[seq_index]
        factors = mem_factor[seq_index]
        live = offset < counts[stretch_of]
        bias = jnp.where(live, jnp.log(factors[stretch_of].astype(jnp.float32)), jnp.float32(-1e9))
        full_bias = jnp.concatenate([jnp.zeros((LEN,), jnp.float32), bias])
        score = jnp.dot(query[seq_index, head_index], all_keys.T, preferred_element_type=jnp.float32) * scale + full_bias[None, :]
        top = jnp.max(score, axis=1, keepdims=True)
        prob = jnp.exp(score - top)
        total = jnp.sum(prob, axis=1, keepdims=True)
        weight = prob.astype(jnp.bfloat16)
        attended = jnp.dot(weight, all_vals, preferred_element_type=jnp.float32) / total
        return attended.astype(jnp.bfloat16)

    attended = lax.map(one_group, jnp.arange(SEQS * HEADS).astype(jnp.int32))
    attended = attended.reshape(SEQS, HEADS, LEN, HD)
    proj = out_weight.reshape(HEADS, HD, D).astype(jnp.float32)
    mixed = jnp.einsum("shld,hde->sle", attended.astype(jnp.float32), proj)
    return mixed.astype(jnp.bfloat16)
```

```python
import functools
import math

import jax
import jax.numpy as jnp
from jax import lax
from jax.experimental import pallas as pl
from jax.experimental.pallas import tpu as pltpu
from jax.sharding import PartitionSpec as P

MCAP = 256


def per_device(query, key, value, mem_key, mem_value, mem_count, mem_factor, out_weight):
    seqs, heads, rows, width = query.shape
    slots_dev = mem_key.shape[2]
    devices = lax.axis_size("seq")
    groups = seqs * heads
    copies = devices // groups
    half = rows // copies
    feat = out_weight.shape[1]
    own_queries = (
        query.reshape(groups, half, copies, width)
        .transpose(0, 2, 1, 3)
        .reshape(groups * copies, half, width)
    )

    def spread(array, count):
        widened = jnp.broadcast_to(
            array.reshape(groups, 1, count, width), (groups, copies, count, width)
        )
        return widened.reshape(groups * copies, count, width)

    head_q, head_k, head_v, head_mk, head_mv = (
        lax.all_to_all(own_queries, "seq", split_axis=0, concat_axis=1, tiled=True),
        lax.all_to_all(spread(key, rows), "seq", split_axis=0, concat_axis=1, tiled=True),
        lax.all_to_all(spread(value, rows), "seq", split_axis=0, concat_axis=1, tiled=True),
        lax.all_to_all(spread(mem_key, slots_dev), "seq", split_axis=0, concat_axis=1, tiled=True),
        lax.all_to_all(
            spread(mem_value, slots_dev), "seq", split_axis=0, concat_axis=1, tiled=True
        ),
    )
    length_q = head_q.shape[1]
    length = head_k.shape[1]
    slots = head_mk.shape[1]
    seq_index = lax.axis_index("seq") // copies // heads
    counts = lax.dynamic_index_in_dim(mem_count, seq_index, 0, keepdims=False)
    factors = lax.dynamic_index_in_dim(mem_factor, seq_index, 0, keepdims=False)
    slot = jnp.arange(slots)
    stretch_of = slot // MCAP
    offset = slot % MCAP
    picked = stretch_of[:, None] == jnp.arange(counts.shape[0])[None, :]
    slot_count = jnp.sum(jnp.where(picked, counts[None, :], 0), 1)
    slot_factor = jnp.sum(jnp.where(picked, factors[None, :], 0), 1)
    bias = jnp.where(
        offset < slot_count, jnp.log(slot_factor.astype(jnp.float32)), jnp.float32(-1000000000.0)
    )
    full_bias = jnp.concatenate([jnp.zeros((length,), jnp.float32), bias])
    all_keys = jnp.concatenate([head_k[0], head_mk[0]], 0)
    all_vals = jnp.concatenate([head_v[0], head_mv[0]], 0)
    scale = width ** (-0.5)
    block = min(512, length_q)
    query_blocks = head_q[0].reshape(length_q // block, block, width)

    def attend(queries):
        score = (
            jnp.einsum("qd,kd->qk", queries, all_keys, preferred_element_type=jnp.float32) * scale
        )
        score = score + full_bias[None, :]
        top = jnp.max(score, axis=1, keepdims=True)
        prob = jnp.exp(score - top)
        total = jnp.sum(prob, axis=1, keepdims=True)
        weight = prob.astype(jnp.bfloat16)
        attended = jnp.dot(weight, all_vals, preferred_element_type=jnp.float32) / total
        return attended.astype(jnp.bfloat16)

    attended = lax.map(attend, query_blocks).reshape(1, length_q, width)
    returned = lax.all_to_all(attended, "seq", split_axis=1, concat_axis=0, tiled=True)
    columns = returned.reshape(seqs, heads, copies, half, width).transpose(0, 3, 2, 1, 4)
    columns = columns.reshape(seqs * rows, heads * width)
    mixed = jnp.dot(
        columns,
        lax.all_gather(out_weight, "seq", axis=0, tiled=True),
        preferred_element_type=jnp.float32,
    )
    result = mixed.reshape(seqs, rows, feat).astype(jnp.bfloat16)
    return result


def exchange_attend(n, scale2, q_hbm, k_hbm, v_hbm, mk_hbm, mv_hbm, bias_ref, out_ref,
                    qbuf, kbuf, vbuf, att, in_send, in_recv, own_sem, ret_send, ret_recv):
    me = lax.axis_index("seq")
    rows, width = qbuf.shape[1], qbuf.shape[2]

    barrier = pltpu.get_barrier_semaphore()

    @pl.loop(1, n)
    def _(step):
        pl.semaphore_signal(barrier, inc=1, device_id={"seq": lax.rem(me + step, n)},
                            device_id_type=pl.DeviceIdType.MESH)

    pl.semaphore_wait(barrier, n - 1)

    streams = (
        (q_hbm, qbuf, 0), (k_hbm, kbuf, 0), (mk_hbm, kbuf, n), (v_hbm, vbuf, 0), (mv_hbm, vbuf, n),
    )

    def sending(a, peer):
        src, dst, base = streams[a]
        return pltpu.make_async_remote_copy(
            src_ref=src.at[0, peer], dst_ref=dst.at[base + me],
            send_sem=in_send.at[a, peer], recv_sem=in_recv.at[a, me],
            device_id={"seq": peer}, device_id_type=pl.DeviceIdType.MESH)

    def arriving(a, peer):
        src, dst, base = streams[a]
        return pltpu.make_async_remote_copy(
            src_ref=src.at[0, peer], dst_ref=dst.at[base + peer],
            send_sem=in_send.at[a, peer], recv_sem=in_recv.at[a, peer],
            device_id={"seq": peer}, device_id_type=pl.DeviceIdType.MESH)

    def own(a):
        src, dst, base = streams[a]
        return pltpu.make_async_copy(src.at[0, me], dst.at[base + me], own_sem.at[a])

    for group in ((0, 1, 2), (3, 4)):
        @pl.loop(0, n - 1)
        def _(k):
            peer = lax.rem(me + 1 + lax.rem(k + n // 2 - 1, n - 1), n)
            for a in group:
                sending(a, peer).start()
    for a in range(5):
        own(a).start()
    for a in range(5):
        own(a).wait()

    @pl.loop(1, n)
    def _(step):
        peer = lax.rem(me + step, n)
        for a in range(5):
            arriving(a, peer).wait_recv()

    keys = kbuf[...].reshape(2 * n * rows, width)
    vals = vbuf[...].reshape(2 * n * rows, width)
    parts = n // 4

    def returning(owner):
        return pltpu.make_async_remote_copy(
            src_ref=att.at[owner],
            dst_ref=out_ref.at[:, pl.ds(pl.multiple_of(me * width, width), width)],
            send_sem=ret_send.at[owner], recv_sem=ret_recv.at[me],
            device_id={"seq": owner}, device_id_type=pl.DeviceIdType.MESH)

    @pl.loop(0, parts)
    def _(j):
        block = lax.rem(me // 4 + parts // 2 + j, parts)
        queries = qbuf[pl.ds(block * 4, 4)].reshape(4 * rows, width)
        score = lax.dot_general(queries, keys, (((1,), (1,)), ((), ())),
                                preferred_element_type=jnp.float32)
        score = score * scale2 + bias_ref[...]
        top = jnp.max(score, axis=1, keepdims=True)
        prob = jnp.exp2(score - top)
        total = jnp.sum(prob, axis=1, keepdims=True)
        mixed = jnp.dot(prob.astype(jnp.bfloat16), vals, preferred_element_type=jnp.float32)
        att[pl.ds(block * 4, 4)] = (mixed / total).astype(jnp.bfloat16).reshape(4, rows, width)
        for t in range(4):
            owner = block * 4 + t

            @pl.when(owner != me)
            def _():
                returning(owner).start()

    mine = pltpu.make_async_copy(
        att.at[me], out_ref.at[:, pl.ds(pl.multiple_of(me * width, width), width)], own_sem.at[0])
    mine.start()
    mine.wait()

    @pl.loop(1, n)
    def _(step):
        peer = lax.rem(me + step, n)
        for a in range(5):
            sending(a, peer).wait_send()
        returning(peer).wait_send()
        pltpu.make_async_remote_copy(
            src_ref=att.at[peer],
            dst_ref=out_ref.at[:, pl.ds(pl.multiple_of(peer * width, width), width)],
            send_sem=ret_send.at[peer], recv_sem=ret_recv.at[peer],
            device_id={"seq": peer}, device_id_type=pl.DeviceIdType.MESH).wait_recv()


def full_bias_of(counts, factors, length, slots):
    slot = jnp.arange(slots)
    picked = (slot // MCAP)[:, None] == jnp.arange(counts.shape[0])[None, :]
    slot_count = jnp.sum(jnp.where(picked, counts[None, :], 0), 1)
    slot_factor = jnp.sum(jnp.where(picked, factors[None, :], 0), 1)
    bias = jnp.where(slot % MCAP < slot_count, jnp.log(slot_factor.astype(jnp.float32)),
                     jnp.float32(-1000000000.0))
    return jnp.concatenate([jnp.zeros((length,), jnp.float32), bias])[None, :]


def per_device_direct(query, key, value, mem_key, mem_value, mem_count, mem_factor, out_weight):
    _, heads, rows, width = query.shape
    n = heads
    log2e = math.log2(math.e)
    bias = full_bias_of(mem_count[0], mem_factor[0], n * rows, n * rows) * log2e
    weights = lax.all_gather(out_weight, "seq", axis=0, tiled=True)
    columns = pl.pallas_call(
        functools.partial(exchange_attend, n, width ** (-0.5) * log2e),
        out_shape=jax.ShapeDtypeStruct((rows, heads * width), query.dtype),
        in_specs=[pl.BlockSpec(memory_space=pl.ANY)] * 5 + [pl.BlockSpec(memory_space=pltpu.VMEM)],
        out_specs=pl.BlockSpec(memory_space=pltpu.VMEM),
        scratch_shapes=[
            pltpu.VMEM((n, rows, width), query.dtype),
            pltpu.VMEM((2 * n, rows, width), query.dtype),
            pltpu.VMEM((2 * n, rows, width), query.dtype),
            pltpu.VMEM((n, rows, width), query.dtype),
            pltpu.SemaphoreType.DMA((5, n)),
            pltpu.SemaphoreType.DMA((5, n)),
            pltpu.SemaphoreType.DMA((5,)),
            pltpu.SemaphoreType.DMA((n,)),
            pltpu.SemaphoreType.DMA((n,)),
        ],
        compiler_params=pltpu.CompilerParams(
            collective_id=0, has_side_effects=True, vmem_limit_bytes=32 << 20),
    )(query, key, value, mem_key, mem_value, bias)
    mixed = jnp.dot(columns, weights, preferred_element_type=jnp.float32)
    return mixed.astype(query.dtype)[None]


def solution(mesh):
    in_specs = (
        P("grp", None, "seq", None),
        P("grp", None, "seq", None),
        P("grp", None, "seq", None),
        P("grp", None, "seq", None),
        P("grp", None, "seq", None),
        P("grp", None),
        P("grp", None),
        P("seq", None),
    )
    out_specs = P("grp", "seq", None)

    def program(query, key, value, mem_key, mem_value, mem_count, mem_factor, out_weight):
        direct = (
            query.shape[0] == mesh.shape["grp"]
            and query.shape[1] == mesh.shape["seq"]
            and query.shape[1] % 8 == 0
            and query.shape[2] == mem_key.shape[2]
            and (query.shape[2] // mesh.shape["seq"]) % 16 == 0
        )
        body = per_device_direct if direct else per_device
        return jax.shard_map(
            body, mesh=mesh, in_specs=in_specs, out_specs=out_specs, check_vma=False
        )(query, key, value, mem_key, mem_value, mem_count, mem_factor, out_weight)

    return program
```

```python
import functools
import math

import jax
import jax.numpy as jnp
from jax import lax
from jax.experimental import pallas as pl
from jax.experimental.pallas import tpu as pltpu
from jax.sharding import PartitionSpec as P

MCAP = 256


def per_device(query, key, value, mem_key, mem_value, mem_count, mem_factor, out_weight):
    seqs, heads, rows, width = query.shape
    slots_dev = mem_key.shape[2]
    devices = lax.axis_size("seq")
    groups = seqs * heads
    copies = devices // groups
    half = rows // copies
    feat = out_weight.shape[1]
    own_queries = (
        query.reshape(groups, half, copies, width)
        .transpose(0, 2, 1, 3)
        .reshape(groups * copies, half, width)
    )

    def spread(array, count):
        widened = jnp.broadcast_to(
            array.reshape(groups, 1, count, width), (groups, copies, count, width)
        )
        return widened.reshape(groups * copies, count, width)

    head_q, head_k, head_v, head_mk, head_mv = (
        lax.all_to_all(own_queries, "seq", split_axis=0, concat_axis=1, tiled=True),
        lax.all_to_all(spread(key, rows), "seq", split_axis=0, concat_axis=1, tiled=True),
        lax.all_to_all(spread(value, rows), "seq", split_axis=0, concat_axis=1, tiled=True),
        lax.all_to_all(spread(mem_key, slots_dev), "seq", split_axis=0, concat_axis=1, tiled=True),
        lax.all_to_all(
            spread(mem_value, slots_dev), "seq", split_axis=0, concat_axis=1, tiled=True
        ),
    )
    length_q = head_q.shape[1]
    length = head_k.shape[1]
    slots = head_mk.shape[1]
    seq_index = lax.axis_index("seq") // copies // heads
    counts = lax.dynamic_index_in_dim(mem_count, seq_index, 0, keepdims=False)
    factors = lax.dynamic_index_in_dim(mem_factor, seq_index, 0, keepdims=False)
    slot = jnp.arange(slots)
    stretch_of = slot // MCAP
    offset = slot % MCAP
    picked = stretch_of[:, None] == jnp.arange(counts.shape[0])[None, :]
    slot_count = jnp.sum(jnp.where(picked, counts[None, :], 0), 1)
    slot_factor = jnp.sum(jnp.where(picked, factors[None, :], 0), 1)
    bias = jnp.where(
        offset < slot_count, jnp.log(slot_factor.astype(jnp.float32)), jnp.float32(-1000000000.0)
    )
    full_bias = jnp.concatenate([jnp.zeros((length,), jnp.float32), bias])
    all_keys = jnp.concatenate([head_k[0], head_mk[0]], 0)
    all_vals = jnp.concatenate([head_v[0], head_mv[0]], 0)
    scale = width ** (-0.5)
    block = min(512, length_q)
    query_blocks = head_q[0].reshape(length_q // block, block, width)

    def attend(queries):
        score = (
            jnp.einsum("qd,kd->qk", queries, all_keys, preferred_element_type=jnp.float32) * scale
        )
        score = score + full_bias[None, :]
        top = jnp.max(score, axis=1, keepdims=True)
        prob = jnp.exp(score - top)
        total = jnp.sum(prob, axis=1, keepdims=True)
        weight = prob.astype(jnp.bfloat16)
        attended = jnp.dot(weight, all_vals, preferred_element_type=jnp.float32) / total
        return attended.astype(jnp.bfloat16)

    attended = lax.map(attend, query_blocks).reshape(1, length_q, width)
    returned = lax.all_to_all(attended, "seq", split_axis=1, concat_axis=0, tiled=True)
    columns = returned.reshape(seqs, heads, copies, half, width).transpose(0, 3, 2, 1, 4)
    columns = columns.reshape(seqs * rows, heads * width)
    mixed = jnp.dot(
        columns,
        lax.all_gather(out_weight, "seq", axis=0, tiled=True),
        preferred_element_type=jnp.float32,
    )
    result = mixed.reshape(seqs, rows, feat).astype(jnp.bfloat16)
    return result


def block_kernel(n, nz, scale2, q_hbm, k_hbm, v_hbm, mk_hbm, mv_hbm, w_hbm, bias_ref, out_ref,
                 qbuf, kbuf, vbuf, att, wbuf, cols, mine, theirs, landed,
                 in_send, in_recv, own_sem, w_sem, sib_send, sib_recv, up_send, up_recv,
                 y_send, y_recv, core_send, core_recv, ret_send, ret_recv, out_send, out_recv):
    me = lax.axis_index("seq")
    g = lax.axis_index("grp")
    plane = n // nz
    z, x, c = me // plane, lax.rem(me // 2, 2), lax.rem(me, 2)
    rows, width = qbuf.shape[1], qbuf.shape[2]
    sibling = me + 1 - 2 * c
    across = me + 2 - 4 * x
    mesh_id = pl.DeviceIdType.MESH

    barrier = pltpu.get_barrier_semaphore()

    @pl.loop(1, n)
    def _(step):
        pl.semaphore_signal(barrier, inc=1, device_id={"seq": lax.rem(me + step, n)},
                            device_id_type=mesh_id)

    pl.semaphore_signal(barrier, inc=1, device_id={"grp": 1 - g}, device_id_type=mesh_id)
    pl.semaphore_wait(barrier, n)

    streams = (
        (q_hbm, qbuf, 0), (k_hbm, kbuf, 0), (mk_hbm, kbuf, n), (v_hbm, vbuf, 0), (mv_hbm, vbuf, n),
    )

    def moving(a, peer, lands):
        src, dst, base = streams[a]
        return pltpu.make_async_remote_copy(
            src_ref=src.at[0, peer], dst_ref=dst.at[base + lands],
            send_sem=in_send.at[a, peer], recv_sem=in_recv.at[a, lands],
            device_id={"seq": peer}, device_id_type=mesh_id)

    def own(a):
        src, dst, base = streams[a]
        return pltpu.make_async_copy(src.at[0, me], dst.at[base + me], own_sem.at[a])

    def wait_inputs(group):
        for a in group:
            own(a).wait()

        @pl.loop(1, n)
        def _(step):
            peer = lax.rem(me + step, n)
            for a in group:
                moving(a, peer, peer).wait_recv()

    def along(d, level, from_own):
        slot = level * 2 + c
        return pltpu.make_async_remote_copy(
            src_ref=w_hbm.at[g] if from_own else wbuf.at[slot, g], dst_ref=wbuf.at[slot, g],
            send_sem=up_send.at[level], recv_sem=up_recv.at[level],
            device_id={"seq": lax.rem(me + d * plane + n, n)}, device_id_type=mesh_id)

    def along_own(i, d):
        return pltpu.make_async_remote_copy(
            src_ref=w_hbm.at[g], dst_ref=wbuf.at[z * 2 + c, g],
            send_sem=up_send.at[nz + i], recv_sem=up_recv.at[z],
            device_id={"seq": lax.rem(me + d * plane + n, n)}, device_id_type=mesh_id)

    def over_y(level, half):
        slot = level * 2 + c
        return pltpu.make_async_remote_copy(
            src_ref=wbuf.at[slot, half], dst_ref=wbuf.at[slot, half],
            send_sem=y_send.at[level], recv_sem=y_recv.at[level],
            device_id={"grp": 1 - g}, device_id_type=mesh_id)

    def over_core(level, half, core):
        slot = level * 2 + core
        return pltpu.make_async_remote_copy(
            src_ref=wbuf.at[slot, half], dst_ref=wbuf.at[slot, half],
            send_sem=core_send.at[level, half], recv_sem=core_recv.at[level, half],
            device_id={"seq": sibling}, device_id_type=mesh_id)

    def to_sibling(core):
        return pltpu.make_async_remote_copy(
            src_ref=w_hbm, dst_ref=wbuf.at[z * 2 + core], send_sem=sib_send, recv_sem=sib_recv,
            device_id={"seq": sibling}, device_id_type=mesh_id)

    def each_level(s, act):
        for d in (1, -1):
            level = z - d * s

            @pl.when((level >= 0) & (level < nz))
            def _():
                act(d, level)

    def each_forward(s, act):
        for d in (1, -1):
            level = z - d * s

            @pl.when((level >= 0) & (level < nz) & (z + d >= 0) & (z + d < nz))
            def _():
                act(d, level)

    def take_chain(s):
        each_level(s, lambda d, level: along(d, level, False).wait_recv())
        if s < nz - 1:
            each_forward(s, lambda d, level: along(d, level, False).start())
        each_level(s, lambda d, level: over_y(level, g).start())
        each_level(s, lambda d, level: over_core(level, g, c).start())

    def take_y(s):
        def act(d, level):
            over_y(level, 1 - g).wait_recv()
            over_core(level, 1 - g, c).start()
        each_level(s, act)

    for group in ((0, 1, 2), (3, 4)):
        @pl.loop(0, n - 1)
        def _(k):
            peer = lax.rem(me + 1 + lax.rem(k + n // 2 - 1, n - 1), n)
            for a in group:
                moving(a, peer, me).start()
    for i, d in enumerate((1, -1)):
        @pl.when((z + d >= 0) & (z + d < nz))
        def _():
            along_own(i, d).start()
    to_sibling(c).start()
    for a in range(5):
        own(a).start()
    own_weight = pltpu.make_async_copy(w_hbm, wbuf.at[z * 2 + c], w_sem)
    own_weight.start()

    take_chain(1)
    wait_inputs((0, 1, 2))
    take_chain(2)
    take_y(1)
    wait_inputs((3, 4))

    keys = kbuf[...].reshape(2 * n * rows, width)
    vals = vbuf[...].reshape(2 * n * rows, width)
    head = z * 2 + c

    def lanes(h):
        return pl.ds(pl.multiple_of(h * width, width), width)

    def returning(level, xr, core):
        owner = level * plane + xr * 2 + core
        return pltpu.make_async_remote_copy(
            src_ref=att.at[owner], dst_ref=cols.at[lax.rem(xr + x, 2), :, lanes(head)],
            send_sem=ret_send.at[owner], recv_sem=ret_recv.at[lax.rem(xr + x, 2), head],
            device_id={"seq": level * plane + x * 2 + core}, device_id_type=mesh_id)

    @pl.loop(0, nz)
    def _(j):
        level = lax.rem(z + nz // 2 + j, nz)
        queries = qbuf[pl.ds(level * plane, plane)].reshape(plane * rows, width)
        score = lax.dot_general(queries, keys, (((1,), (1,)), ((), ())),
                                preferred_element_type=jnp.float32)
        score = score * scale2 + bias_ref[...]
        top = jnp.max(score, axis=1, keepdims=True)
        prob = jnp.exp2(score - top)
        total = jnp.sum(prob, axis=1, keepdims=True)
        mixed = jnp.dot(prob.astype(jnp.bfloat16), vals, preferred_element_type=jnp.float32)
        att[pl.ds(level * plane, plane)] = (
            (mixed / total).astype(jnp.bfloat16).reshape(plane, rows, width))
        for core in range(2):
            for xr in range(2):
                @pl.when((level != z) | (core != c))
                def _():
                    returning(level, xr, core).start()

    for xr in range(2):
        keep = pltpu.make_async_copy(
            att.at[z * plane + xr * 2 + c], cols.at[lax.rem(xr + x, 2), :, lanes(head)],
            own_sem.at[xr])
        keep.start()
        keep.wait()

    take_chain(3)
    take_y(2)
    take_y(3)
    own_weight.wait()
    to_sibling(1 - c).wait_recv()

    def last_core(d, level):
        for half in range(2):
            over_core(level, half, 1 - c).wait_recv()

    for s in range(1, nz):
        each_level(s, last_core)

    @pl.loop(0, 2 * nz)
    def _(h):
        for slot in range(2):
            @pl.when(h != head)
            def _():
                pltpu.make_async_remote_copy(
                    src_ref=att.at[0], dst_ref=cols.at[slot, :, lanes(h)],
                    send_sem=ret_send.at[0], recv_sem=ret_recv.at[slot, h],
                    device_id={"seq": sibling}, device_id_type=mesh_id).wait_recv()

    tiles, tile = landed.shape[0], landed.shape[2]
    left = jnp.concatenate([cols[0], cols[1]], 0)

    def crossing(t):
        return pltpu.make_async_remote_copy(
            src_ref=theirs.at[t], dst_ref=landed.at[t],
            send_sem=out_send.at[t], recv_sem=out_recv.at[t],
            device_id={"seq": across}, device_id_type=mesh_id)

    for t in range(tiles):
        right = wbuf[:, :, :, t * tile:(t + 1) * tile].reshape(2 * nz * width, tile)
        mixed = jnp.dot(left, right, preferred_element_type=jnp.float32)
        theirs[t] = mixed[rows:].astype(jnp.bfloat16)
        crossing(t).start()
        mine[t] = mixed[:rows]
    for t in range(tiles):
        crossing(t).wait_recv()
        out_ref[:, t * tile:(t + 1) * tile] = (
            mine[t] + landed[t].astype(jnp.float32)).astype(out_ref.dtype)

    @pl.loop(1, n)
    def _(step):
        peer = lax.rem(me + step, n)
        for a in range(5):
            moving(a, peer, me).wait_send()

    @pl.loop(0, nz)
    def _(level):
        for core in range(2):
            for xr in range(2):
                @pl.when((level != z) | (core != c))
                def _():
                    returning(level, xr, core).wait_send()

    for i, d in enumerate((1, -1)):
        @pl.when((z + d >= 0) & (z + d < nz))
        def _():
            along_own(i, d).wait_send()
    for s in range(1, nz - 1):
        each_forward(s, lambda d, level: along(d, level, False).wait_send())
    for s in range(1, nz):
        each_level(s, lambda d, level: over_y(level, g).wait_send())
        each_level(s, lambda d, level: over_core(level, 0, c).wait_send())
        each_level(s, lambda d, level: over_core(level, 1, c).wait_send())
    to_sibling(c).wait_send()
    for t in range(tiles):
        crossing(t).wait_send()


def full_bias_of(counts, factors, length, slots):
    slot = jnp.arange(slots)
    picked = (slot // MCAP)[:, None] == jnp.arange(counts.shape[0])[None, :]
    slot_count = jnp.sum(jnp.where(picked, counts[None, :], 0), 1)
    slot_factor = jnp.sum(jnp.where(picked, factors[None, :], 0), 1)
    bias = jnp.where(slot % MCAP < slot_count, jnp.log(slot_factor.astype(jnp.float32)),
                     jnp.float32(-1000000000.0))
    return jnp.concatenate([jnp.zeros((length,), jnp.float32), bias])[None, :]


def per_device_direct(query, key, value, mem_key, mem_value, mem_count, mem_factor, out_weight):
    _, heads, rows, width = query.shape
    n = heads
    log2e = math.log2(math.e)
    bias = full_bias_of(mem_count[0], mem_factor[0], n * rows, n * rows) * log2e
    depth, feat = out_weight.shape
    nz = n // 4
    tile = 512
    bf16 = query.dtype
    dma = pltpu.SemaphoreType.DMA
    result = pl.pallas_call(
        functools.partial(block_kernel, n, nz, width ** (-0.5) * log2e),
        out_shape=jax.ShapeDtypeStruct((rows, feat), bf16),
        in_specs=[pl.BlockSpec(memory_space=pltpu.HBM)] * 6 + [pl.BlockSpec(memory_space=pltpu.VMEM)],
        out_specs=pl.BlockSpec(memory_space=pltpu.VMEM),
        scratch_shapes=[
            pltpu.VMEM((n, rows, width), bf16),
            pltpu.VMEM((2 * n, rows, width), bf16),
            pltpu.VMEM((2 * n, rows, width), bf16),
            pltpu.VMEM((n, rows, width), bf16),
            pltpu.VMEM((2 * nz, 2, depth // 2, feat), bf16),
            pltpu.VMEM((2, rows, 2 * nz * width), bf16),
            pltpu.VMEM((feat // tile, rows, tile), jnp.float32),
            pltpu.VMEM((feat // tile, rows, tile), bf16),
            pltpu.VMEM((feat // tile, rows, tile), bf16),
            dma((5, n)), dma((5, n)), dma((5,)), dma, dma, dma, dma((nz + 2,)), dma((nz,)),
            dma((nz,)), dma((nz,)), dma((nz, 2)), dma((nz, 2)), dma((n,)), dma((2, 2 * nz)),
            dma((feat // tile,)), dma((feat // tile,)),
        ],
        compiler_params=pltpu.CompilerParams(
            collective_id=0, has_side_effects=True, vmem_limit_bytes=62 << 20),
    )(query, key, value, mem_key, mem_value, out_weight.reshape(2, depth // 2, feat), bias)
    return result[None]


def solution(mesh):
    in_specs = (
        P("grp", None, "seq", None),
        P("grp", None, "seq", None),
        P("grp", None, "seq", None),
        P("grp", None, "seq", None),
        P("grp", None, "seq", None),
        P("grp", None),
        P("grp", None),
        P("seq", None),
    )
    out_specs = P("grp", "seq", None)

    def program(query, key, value, mem_key, mem_value, mem_count, mem_factor, out_weight):
        direct = (
            query.shape[0] == mesh.shape["grp"]
            and query.shape[1] == mesh.shape["seq"]
            and mesh.shape["grp"] == 2
            and query.shape[1] == 16
            and out_weight.shape[0] == query.shape[1] * query.shape[3]
            and query.shape[3] == 128
            and out_weight.shape[1] % 512 == 0
            and query.shape[2] == mem_key.shape[2]
            and (query.shape[2] // mesh.shape["seq"]) % 16 == 0
        )
        body = per_device_direct if direct else per_device
        return jax.shard_map(
            body, mesh=mesh, in_specs=in_specs, out_specs=out_specs, check_vma=False
        )(query, key, value, mem_key, mem_value, mem_count, mem_factor, out_weight)

    return program
```

```python
import functools
import math

import jax
import jax.numpy as jnp
from jax import lax
from jax.experimental import pallas as pl
from jax.experimental.pallas import tpu as pltpu
from jax.sharding import PartitionSpec as P

MCAP = 256


def per_device(query, key, value, mem_key, mem_value, mem_count, mem_factor, out_weight):
    seqs, heads, rows, width = query.shape
    slots_dev = mem_key.shape[2]
    devices = lax.axis_size("seq")
    groups = seqs * heads
    copies = devices // groups
    half = rows // copies
    feat = out_weight.shape[1]
    own_queries = (
        query.reshape(groups, half, copies, width)
        .transpose(0, 2, 1, 3)
        .reshape(groups * copies, half, width)
    )

    def spread(array, count):
        widened = jnp.broadcast_to(
            array.reshape(groups, 1, count, width), (groups, copies, count, width)
        )
        return widened.reshape(groups * copies, count, width)

    head_q, head_k, head_v, head_mk, head_mv = (
        lax.all_to_all(own_queries, "seq", split_axis=0, concat_axis=1, tiled=True),
        lax.all_to_all(spread(key, rows), "seq", split_axis=0, concat_axis=1, tiled=True),
        lax.all_to_all(spread(value, rows), "seq", split_axis=0, concat_axis=1, tiled=True),
        lax.all_to_all(spread(mem_key, slots_dev), "seq", split_axis=0, concat_axis=1, tiled=True),
        lax.all_to_all(
            spread(mem_value, slots_dev), "seq", split_axis=0, concat_axis=1, tiled=True
        ),
    )
    length_q = head_q.shape[1]
    length = head_k.shape[1]
    slots = head_mk.shape[1]
    seq_index = lax.axis_index("seq") // copies // heads
    counts = lax.dynamic_index_in_dim(mem_count, seq_index, 0, keepdims=False)
    factors = lax.dynamic_index_in_dim(mem_factor, seq_index, 0, keepdims=False)
    slot = jnp.arange(slots)
    stretch_of = slot // MCAP
    offset = slot % MCAP
    picked = stretch_of[:, None] == jnp.arange(counts.shape[0])[None, :]
    slot_count = jnp.sum(jnp.where(picked, counts[None, :], 0), 1)
    slot_factor = jnp.sum(jnp.where(picked, factors[None, :], 0), 1)
    bias = jnp.where(
        offset < slot_count, jnp.log(slot_factor.astype(jnp.float32)), jnp.float32(-1000000000.0)
    )
    full_bias = jnp.concatenate([jnp.zeros((length,), jnp.float32), bias])
    all_keys = jnp.concatenate([head_k[0], head_mk[0]], 0)
    all_vals = jnp.concatenate([head_v[0], head_mv[0]], 0)
    scale = width ** (-0.5)
    block = min(512, length_q)
    query_blocks = head_q[0].reshape(length_q // block, block, width)

    def attend(queries):
        score = (
            jnp.einsum("qd,kd->qk", queries, all_keys, preferred_element_type=jnp.float32) * scale
        )
        score = score + full_bias[None, :]
        top = jnp.max(score, axis=1, keepdims=True)
        prob = jnp.exp(score - top)
        total = jnp.sum(prob, axis=1, keepdims=True)
        weight = prob.astype(jnp.bfloat16)
        attended = jnp.dot(weight, all_vals, preferred_element_type=jnp.float32) / total
        return attended.astype(jnp.bfloat16)

    attended = lax.map(attend, query_blocks).reshape(1, length_q, width)
    returned = lax.all_to_all(attended, "seq", split_axis=1, concat_axis=0, tiled=True)
    columns = returned.reshape(seqs, heads, copies, half, width).transpose(0, 3, 2, 1, 4)
    columns = columns.reshape(seqs * rows, heads * width)
    mixed = jnp.dot(
        columns,
        lax.all_gather(out_weight, "seq", axis=0, tiled=True),
        preferred_element_type=jnp.float32,
    )
    result = mixed.reshape(seqs, rows, feat).astype(jnp.bfloat16)
    return result


LOG2E = math.log2(math.e)
PIECES = 2


def block_kernel(n, nz, scale2, q_hbm, k_hbm, v_hbm, mk_hbm, mv_hbm, w_hbm, count_ref, factor_ref, out_ref,
                 qbuf, kbuf, vbuf, att, wbuf, cols, mine, theirs, landed, bias_ref,
                 in_send, in_recv, own_sem, w_sem, sib_send, sib_recv, up_send, up_recv,
                 y_send, y_recv, core_send, core_recv, ret_send, ret_recv, out_send, out_recv):
    me = lax.axis_index("seq")
    g = lax.axis_index("grp")
    plane = n // nz
    z, x, c = me // plane, lax.rem(me // 2, 2), lax.rem(me, 2)
    rows, width = qbuf.shape[1], qbuf.shape[2]
    sibling = me + 1 - 2 * c
    across = me + 2 - 4 * x
    mesh_id = pl.DeviceIdType.MESH

    barrier = pltpu.get_barrier_semaphore()

    @pl.loop(1, n)
    def _(step):
        pl.semaphore_signal(barrier, inc=1, device_id={"seq": lax.rem(me + step, n)},
                            device_id_type=mesh_id)

    pl.semaphore_signal(barrier, inc=1, device_id={"grp": 1 - g}, device_id_type=mesh_id)
    pl.semaphore_wait(barrier, n)

    streams = (
        (q_hbm, qbuf, 0), (k_hbm, kbuf, 0), (mk_hbm, kbuf, n), (v_hbm, vbuf, 0), (mv_hbm, vbuf, n),
    )

    def moving(a, peer, lands):
        src, dst, base = streams[a]
        return pltpu.make_async_remote_copy(
            src_ref=src.at[0, peer], dst_ref=dst.at[base + lands],
            send_sem=in_send.at[a, peer], recv_sem=in_recv.at[a, lands],
            device_id={"seq": peer}, device_id_type=mesh_id)

    def own(a):
        src, dst, base = streams[a]
        return pltpu.make_async_copy(src.at[0, me], dst.at[base + me], own_sem.at[a])

    def wait_inputs(group):
        for a in group:
            own(a).wait()

        @pl.loop(1, n)
        def _(step):
            peer = lax.rem(me + step, n)
            for a in group:
                moving(a, peer, peer).wait_recv()

    pieces, span = wbuf.shape[0], wbuf.shape[4]

    def columns(p):
        return pl.ds(p * span, span)

    def along(d, level, p):
        slot = level * 2 + c
        return pltpu.make_async_remote_copy(
            src_ref=wbuf.at[p, slot, g], dst_ref=wbuf.at[p, slot, g],
            send_sem=up_send.at[level, p], recv_sem=up_recv.at[level, p],
            device_id={"seq": lax.rem(me + d * plane + n, n)}, device_id_type=mesh_id)

    def along_own(i, d, p):
        return pltpu.make_async_remote_copy(
            src_ref=w_hbm.at[g, :, columns(p)], dst_ref=wbuf.at[p, z * 2 + c, g],
            send_sem=up_send.at[nz + i, p], recv_sem=up_recv.at[z, p],
            device_id={"seq": lax.rem(me + d * plane + n, n)}, device_id_type=mesh_id)

    def over_y(level, half, p):
        slot = level * 2 + c
        return pltpu.make_async_remote_copy(
            src_ref=wbuf.at[p, slot, half], dst_ref=wbuf.at[p, slot, half],
            send_sem=y_send.at[level, p], recv_sem=y_recv.at[level, p],
            device_id={"grp": 1 - g}, device_id_type=mesh_id)

    def over_core(level, half, core, p):
        slot = level * 2 + core
        return pltpu.make_async_remote_copy(
            src_ref=wbuf.at[p, slot, half], dst_ref=wbuf.at[p, slot, half],
            send_sem=core_send.at[level, half, p], recv_sem=core_recv.at[level, half, p],
            device_id={"seq": sibling}, device_id_type=mesh_id)

    def to_sibling(core, p):
        return pltpu.make_async_remote_copy(
            src_ref=w_hbm.at[:, :, columns(p)], dst_ref=wbuf.at[p, z * 2 + core],
            send_sem=sib_send.at[p], recv_sem=sib_recv.at[p],
            device_id={"seq": sibling}, device_id_type=mesh_id)

    def own_weight(p):
        return pltpu.make_async_copy(
            w_hbm.at[:, :, columns(p)], wbuf.at[p, z * 2 + c], w_sem.at[p])

    def each_level(s, act):
        for d in (1, -1):
            level = z - d * s

            @pl.when((level >= 0) & (level < nz))
            def _():
                act(d, level)

    def each_forward(s, act):
        for d in (1, -1):
            level = z - d * s

            @pl.when((level >= 0) & (level < nz) & (z + d >= 0) & (z + d < nz))
            def _():
                act(d, level)

    def take_chain(s, p):
        each_level(s, lambda d, level: along(d, level, p).wait_recv())
        if s < nz - 1:
            each_forward(s, lambda d, level: along(d, level, p).start())
        each_level(s, lambda d, level: over_y(level, g, p).start())
        each_level(s, lambda d, level: over_core(level, g, c, p).start())

    def take_y(s, p):
        def act(d, level):
            over_y(level, 1 - g, p).wait_recv()
            over_core(level, 1 - g, c, p).start()
        each_level(s, act)

    for group in ((0, 1, 2), (3, 4)):
        @pl.loop(0, n - 1)
        def _(k):
            peer = lax.rem(me + 1 + lax.rem(k + n // 2 - 1, n - 1), n)
            for a in group:
                moving(a, peer, me).start()
    for i, d in enumerate((1, -1)):
        @pl.when((z + d >= 0) & (z + d < nz))
        def _():
            for p in range(pieces):
                along_own(i, d, p).start()
    for p in range(pieces):
        to_sibling(c, p).start()
    for a in range(5):
        own(a).start()
    for p in range(pieces):
        own_weight(p).start()

    for s in (1, 2):
        for p in range(pieces):
            take_chain(s, p)
    for p in range(pieces):
        take_y(1, p)
    wait_inputs((0, 1, 2, 3, 4))

    slot_at = lax.broadcasted_iota(jnp.int32, (1, MCAP), 1)
    parts = [jnp.zeros((1, n * rows), jnp.float32)]
    for s in range(count_ref.shape[1]):
        factor = jnp.full((1, MCAP), factor_ref[0, s], jnp.int32).astype(jnp.float32)
        parts.append(jnp.where(slot_at < count_ref[0, s], jnp.log(factor) * LOG2E,
                               jnp.float32(-1.0e9)))
    bias_ref[...] = jnp.concatenate(parts, 1)

    keys = kbuf[...].reshape(2 * n * rows, width)
    vals = vbuf[...].reshape(2 * n * rows, width)
    head = z * 2 + c

    def lanes(h):
        return pl.ds(pl.multiple_of(h * width, width), width)

    def returning(level, xr, core):
        owner = level * plane + xr * 2 + core
        return pltpu.make_async_remote_copy(
            src_ref=att.at[owner], dst_ref=cols.at[lax.rem(xr + x, 2), :, lanes(head)],
            send_sem=ret_send.at[owner], recv_sem=ret_recv.at[lax.rem(xr + x, 2), head],
            device_id={"seq": level * plane + x * 2 + core}, device_id_type=mesh_id)

    def attend(j):
        level = lax.rem(z + nz // 2 + j, nz)
        queries = qbuf[pl.ds(level * plane, plane)].reshape(plane * rows, width)
        score = lax.dot_general(queries, keys, (((1,), (1,)), ((), ())),
                                preferred_element_type=jnp.float32)
        score = score * scale2 + bias_ref[...]
        top = jnp.max(score, axis=1, keepdims=True)
        prob = jnp.exp2(score - top)
        total = jnp.sum(prob, axis=1, keepdims=True)
        mixed = jnp.dot(prob.astype(jnp.bfloat16), vals, preferred_element_type=jnp.float32)
        att[pl.ds(level * plane, plane)] = (
            (mixed / total).astype(jnp.bfloat16).reshape(plane, rows, width))
        for core in range(2):
            for xr in range(2):
                @pl.when((level != z) | (core != c))
                def _():
                    returning(level, xr, core).start()

    for j in range(nz):
        attend(j)
        if j == 1:
            take_chain(3, 0)
            take_y(2, 0)
        if j == 2:
            for p in range(1, pieces):
                take_chain(3, p)

    for xr in range(2):
        keep = pltpu.make_async_copy(
            att.at[z * plane + xr * 2 + c], cols.at[lax.rem(xr + x, 2), :, lanes(head)],
            own_sem.at[xr])
        keep.start()
        keep.wait()

    take_y(3, 0)
    for p in range(1, pieces):
        take_y(2, p)

    def last_core(p):
        def act(d, level):
            for half in range(2):
                over_core(level, half, 1 - c, p).wait_recv()
        for s in range(1, nz):
            each_level(s, act)
        own_weight(p).wait()
        to_sibling(1 - c, p).wait_recv()

    @pl.loop(0, 2 * nz)
    def _(h):
        for slot in range(2):
            @pl.when(h != head)
            def _():
                pltpu.make_async_remote_copy(
                    src_ref=att.at[0], dst_ref=cols.at[slot, :, lanes(h)],
                    send_sem=ret_send.at[0], recv_sem=ret_recv.at[slot, h],
                    device_id={"seq": sibling}, device_id_type=mesh_id).wait_recv()

    tiles, tile = landed.shape[0], landed.shape[2]
    left = jnp.concatenate([cols[0], cols[1]], 0)

    def crossing(t):
        return pltpu.make_async_remote_copy(
            src_ref=theirs.at[t], dst_ref=landed.at[t],
            send_sem=out_send.at[t], recv_sem=out_recv.at[t],
            device_id={"seq": across}, device_id_type=mesh_id)

    for t in range(tiles):
        p, first = t * tile // span, t * tile % span
        if first == 0:
            if p:
                take_y(3, p)
            last_core(p)
        right = wbuf[p, :, :, :, first:first + tile].reshape(2 * nz * width, tile)
        mixed = jnp.dot(left, right, preferred_element_type=jnp.float32)
        theirs[t] = mixed[rows:].astype(jnp.bfloat16)
        crossing(t).start()
        mine[t] = mixed[:rows]
    for t in range(tiles):
        crossing(t).wait_recv()
        out_ref[:, t * tile:(t + 1) * tile] = (
            mine[t] + landed[t].astype(jnp.float32)).astype(out_ref.dtype)

    @pl.loop(1, n)
    def _(step):
        peer = lax.rem(me + step, n)
        for a in range(5):
            moving(a, peer, me).wait_send()

    @pl.loop(0, nz)
    def _(level):
        for core in range(2):
            for xr in range(2):
                @pl.when((level != z) | (core != c))
                def _():
                    returning(level, xr, core).wait_send()

    for i, d in enumerate((1, -1)):
        @pl.when((z + d >= 0) & (z + d < nz))
        def _():
            for p in range(pieces):
                along_own(i, d, p).wait_send()

    def sent_on(d, level):
        for p in range(pieces):
            over_y(level, g, p).wait_send()
            over_core(level, 0, c, p).wait_send()
            over_core(level, 1, c, p).wait_send()

    def forwarded(d, level):
        for p in range(pieces):
            along(d, level, p).wait_send()

    for s in range(1, nz - 1):
        each_forward(s, forwarded)
    for s in range(1, nz):
        each_level(s, sent_on)
    for p in range(pieces):
        to_sibling(c, p).wait_send()
    for t in range(tiles):
        crossing(t).wait_send()


def per_device_direct(query, key, value, mem_key, mem_value, mem_count, mem_factor, out_weight):
    _, heads, rows, width = query.shape
    n = heads
    depth, feat = out_weight.shape
    nz = n // 4
    tile = 512
    bf16 = query.dtype
    dma = pltpu.SemaphoreType.DMA
    result = pl.pallas_call(
        functools.partial(block_kernel, n, nz, width ** (-0.5) * LOG2E),
        out_shape=jax.ShapeDtypeStruct((rows, feat), bf16),
        in_specs=[pl.BlockSpec(memory_space=pltpu.HBM)] * 6 + [pl.BlockSpec(memory_space=pltpu.SMEM)] * 2,
        out_specs=pl.BlockSpec(memory_space=pltpu.VMEM),
        scratch_shapes=[
            pltpu.VMEM((n, rows, width), bf16),
            pltpu.VMEM((2 * n, rows, width), bf16),
            pltpu.VMEM((2 * n, rows, width), bf16),
            pltpu.VMEM((n, rows, width), bf16),
            pltpu.VMEM((PIECES, 2 * nz, 2, depth // 2, feat // PIECES), bf16),
            pltpu.VMEM((2, rows, 2 * nz * width), bf16),
            pltpu.VMEM((feat // tile, rows, tile), jnp.float32),
            pltpu.VMEM((feat // tile, rows, tile), bf16),
            pltpu.VMEM((feat // tile, rows, tile), bf16),
            pltpu.VMEM((1, 2 * n * rows), jnp.float32),
            dma((5, n)), dma((5, n)), dma((5,)), dma((PIECES,)), dma((PIECES,)), dma((PIECES,)),
            dma((nz + 2, PIECES)), dma((nz, PIECES)), dma((nz, PIECES)), dma((nz, PIECES)),
            dma((nz, 2, PIECES)), dma((nz, 2, PIECES)), dma((n,)), dma((2, 2 * nz)),
            dma((feat // tile,)), dma((feat // tile,)),
        ],
        compiler_params=pltpu.CompilerParams(
            collective_id=0, has_side_effects=True, vmem_limit_bytes=62 << 20),
    )(query, key, value, mem_key, mem_value, out_weight.reshape(2, depth // 2, feat),
      mem_count, mem_factor)
    return result[None]


def solution(mesh):
    in_specs = (
        P("grp", None, "seq", None),
        P("grp", None, "seq", None),
        P("grp", None, "seq", None),
        P("grp", None, "seq", None),
        P("grp", None, "seq", None),
        P("grp", None),
        P("grp", None),
        P("seq", None),
    )
    out_specs = P("grp", "seq", None)

    def program(query, key, value, mem_key, mem_value, mem_count, mem_factor, out_weight):
        direct = (
            query.shape[0] == mesh.shape["grp"]
            and query.shape[1] == mesh.shape["seq"]
            and mesh.shape["grp"] == 2
            and query.shape[1] == 16
            and out_weight.shape[0] == query.shape[1] * query.shape[3]
            and query.shape[3] == 128
            and out_weight.shape[1] % (512 * PIECES) == 0
            and mem_key.shape[2] == mem_count.shape[1] * MCAP
            and query.shape[2] == mem_key.shape[2]
            and (query.shape[2] // mesh.shape["seq"]) % 16 == 0
        )
        body = per_device_direct if direct else per_device
        return jax.shard_map(
            body, mesh=mesh, in_specs=in_specs, out_specs=out_specs, check_vma=False
        )(query, key, value, mem_key, mem_value, mem_count, mem_factor, out_weight)

    return program
```

```python
import functools
import math

import jax
import jax.numpy as jnp
from jax import lax
from jax.experimental import pallas as pl
from jax.experimental.pallas import tpu as pltpu
from jax.sharding import PartitionSpec as P

MCAP = 256


def per_device(query, key, value, mem_key, mem_value, mem_count, mem_factor, out_weight):
    seqs, heads, rows, width = query.shape
    slots_dev = mem_key.shape[2]
    devices = lax.axis_size("seq")
    groups = seqs * heads
    copies = devices // groups
    half = rows // copies
    feat = out_weight.shape[1]
    own_queries = (
        query.reshape(groups, half, copies, width)
        .transpose(0, 2, 1, 3)
        .reshape(groups * copies, half, width)
    )

    def spread(array, count):
        widened = jnp.broadcast_to(
            array.reshape(groups, 1, count, width), (groups, copies, count, width)
        )
        return widened.reshape(groups * copies, count, width)

    head_q, head_k, head_v, head_mk, head_mv = (
        lax.all_to_all(own_queries, "seq", split_axis=0, concat_axis=1, tiled=True),
        lax.all_to_all(spread(key, rows), "seq", split_axis=0, concat_axis=1, tiled=True),
        lax.all_to_all(spread(value, rows), "seq", split_axis=0, concat_axis=1, tiled=True),
        lax.all_to_all(spread(mem_key, slots_dev), "seq", split_axis=0, concat_axis=1, tiled=True),
        lax.all_to_all(
            spread(mem_value, slots_dev), "seq", split_axis=0, concat_axis=1, tiled=True
        ),
    )
    length_q = head_q.shape[1]
    length = head_k.shape[1]
    slots = head_mk.shape[1]
    seq_index = lax.axis_index("seq") // copies // heads
    counts = lax.dynamic_index_in_dim(mem_count, seq_index, 0, keepdims=False)
    factors = lax.dynamic_index_in_dim(mem_factor, seq_index, 0, keepdims=False)
    slot = jnp.arange(slots)
    stretch_of = slot // MCAP
    offset = slot % MCAP
    picked = stretch_of[:, None] == jnp.arange(counts.shape[0])[None, :]
    slot_count = jnp.sum(jnp.where(picked, counts[None, :], 0), 1)
    slot_factor = jnp.sum(jnp.where(picked, factors[None, :], 0), 1)
    bias = jnp.where(
        offset < slot_count, jnp.log(slot_factor.astype(jnp.float32)), jnp.float32(-1000000000.0)
    )
    full_bias = jnp.concatenate([jnp.zeros((length,), jnp.float32), bias])
    all_keys = jnp.concatenate([head_k[0], head_mk[0]], 0)
    all_vals = jnp.concatenate([head_v[0], head_mv[0]], 0)
    scale = width ** (-0.5)
    block = min(512, length_q)
    query_blocks = head_q[0].reshape(length_q // block, block, width)

    def attend(queries):
        score = (
            jnp.einsum("qd,kd->qk", queries, all_keys, preferred_element_type=jnp.float32) * scale
        )
        score = score + full_bias[None, :]
        top = jnp.max(score, axis=1, keepdims=True)
        prob = jnp.exp(score - top)
        total = jnp.sum(prob, axis=1, keepdims=True)
        weight = prob.astype(jnp.bfloat16)
        attended = jnp.dot(weight, all_vals, preferred_element_type=jnp.float32) / total
        return attended.astype(jnp.bfloat16)

    attended = lax.map(attend, query_blocks).reshape(1, length_q, width)
    returned = lax.all_to_all(attended, "seq", split_axis=1, concat_axis=0, tiled=True)
    columns = returned.reshape(seqs, heads, copies, half, width).transpose(0, 3, 2, 1, 4)
    columns = columns.reshape(seqs * rows, heads * width)
    mixed = jnp.dot(
        columns,
        lax.all_gather(out_weight, "seq", axis=0, tiled=True),
        preferred_element_type=jnp.float32,
    )
    result = mixed.reshape(seqs, rows, feat).astype(jnp.bfloat16)
    return result


LOG2E = math.log2(math.e)
PIECES = 3


def block_kernel(n, nz, scale2, q_hbm, k_hbm, v_hbm, mk_hbm, mv_hbm, w_hbm, count_ref, factor_ref, out_ref,
                 qbuf, kbuf, vbuf, att, wbuf, cols, mine, theirs, landed, bias_ref,
                 in_send, in_recv, own_sem, w_sem, sib_send, sib_recv, up_send, up_recv,
                 y_send, y_recv, core_send, core_recv, ret_send, ret_recv, out_send, out_recv):
    me = lax.axis_index("seq")
    g = lax.axis_index("grp")
    plane = n // nz
    z, x, c = me // plane, lax.rem(me // 2, 2), lax.rem(me, 2)
    rows, width = qbuf.shape[1], qbuf.shape[2]
    sibling = me + 1 - 2 * c
    across = me + 2 - 4 * x
    mesh_id = pl.DeviceIdType.MESH

    barrier = pltpu.get_barrier_semaphore()

    @pl.loop(1, n)
    def _(step):
        pl.semaphore_signal(barrier, inc=1, device_id={"seq": lax.rem(me + step, n)},
                            device_id_type=mesh_id)

    pl.semaphore_signal(barrier, inc=1, device_id={"grp": 1 - g}, device_id_type=mesh_id)
    pl.semaphore_wait(barrier, n)

    streams = (
        (q_hbm, qbuf, 0), (k_hbm, kbuf, 0), (mk_hbm, kbuf, n), (v_hbm, vbuf, 0), (mv_hbm, vbuf, n),
    )

    def moving(a, peer, lands):
        src, dst, base = streams[a]
        return pltpu.make_async_remote_copy(
            src_ref=src.at[0, peer], dst_ref=dst.at[base + lands],
            send_sem=in_send.at[a, peer], recv_sem=in_recv.at[a, lands],
            device_id={"seq": peer}, device_id_type=mesh_id)

    def own(a):
        src, dst, base = streams[a]
        return pltpu.make_async_copy(src.at[0, me], dst.at[base + me], own_sem.at[a])

    def wait_inputs(group):
        for a in group:
            own(a).wait()

        @pl.loop(1, n)
        def _(step):
            peer = lax.rem(me + step, n)
            for a in group:
                moving(a, peer, peer).wait_recv()

    pieces, span = wbuf.shape[0], wbuf.shape[4]

    def columns(p):
        return pl.ds(p * span, span)

    def along(d, level, p):
        slot = level * 2 + c
        return pltpu.make_async_remote_copy(
            src_ref=wbuf.at[p, slot, g], dst_ref=wbuf.at[p, slot, g],
            send_sem=up_send.at[level, p], recv_sem=up_recv.at[level, p],
            device_id={"seq": lax.rem(me + d * plane + n, n)}, device_id_type=mesh_id)

    def along_own(i, d, p):
        return pltpu.make_async_remote_copy(
            src_ref=w_hbm.at[g, :, columns(p)], dst_ref=wbuf.at[p, z * 2 + c, g],
            send_sem=up_send.at[nz + i, p], recv_sem=up_recv.at[z, p],
            device_id={"seq": lax.rem(me + d * plane + n, n)}, device_id_type=mesh_id)

    def over_y(level, half, p):
        slot = level * 2 + c
        return pltpu.make_async_remote_copy(
            src_ref=wbuf.at[p, slot, half], dst_ref=wbuf.at[p, slot, half],
            send_sem=y_send.at[level, p], recv_sem=y_recv.at[level, p],
            device_id={"grp": 1 - g}, device_id_type=mesh_id)

    def over_core(level, half, core, p):
        slot = level * 2 + core
        return pltpu.make_async_remote_copy(
            src_ref=wbuf.at[p, slot, half], dst_ref=wbuf.at[p, slot, half],
            send_sem=core_send.at[level, half, p], recv_sem=core_recv.at[level, half, p],
            device_id={"seq": sibling}, device_id_type=mesh_id)

    def to_sibling(core, p):
        return pltpu.make_async_remote_copy(
            src_ref=w_hbm.at[:, :, columns(p)], dst_ref=wbuf.at[p, z * 2 + core],
            send_sem=sib_send.at[p], recv_sem=sib_recv.at[p],
            device_id={"seq": sibling}, device_id_type=mesh_id)

    def own_weight(p):
        return pltpu.make_async_copy(
            w_hbm.at[:, :, columns(p)], wbuf.at[p, z * 2 + c], w_sem.at[p])

    def each_level(s, act):
        for d in (1, -1):
            level = z - d * s

            @pl.when((level >= 0) & (level < nz))
            def _():
                act(d, level)

    def each_forward(s, act):
        for d in (1, -1):
            level = z - d * s

            @pl.when((level >= 0) & (level < nz) & (z + d >= 0) & (z + d < nz))
            def _():
                act(d, level)

    def take_chain(s, p):
        each_level(s, lambda d, level: along(d, level, p).wait_recv())
        if s < nz - 1:
            each_forward(s, lambda d, level: along(d, level, p).start())
        each_level(s, lambda d, level: over_y(level, g, p).start())
        each_level(s, lambda d, level: over_core(level, g, c, p).start())

    def take_y(s, p):
        def act(d, level):
            over_y(level, 1 - g, p).wait_recv()
            over_core(level, 1 - g, c, p).start()
        each_level(s, act)

    for group in ((0, 1, 2), (3, 4)):
        @pl.loop(0, n - 1)
        def _(k):
            peer = lax.rem(me + 1 + lax.rem(k + n // 2 - 1, n - 1), n)
            for a in group:
                moving(a, peer, me).start()
    for i, d in enumerate((1, -1)):
        @pl.when((z + d >= 0) & (z + d < nz))
        def _():
            for p in range(pieces):
                along_own(i, d, p).start()
    for p in range(pieces):
        to_sibling(c, p).start()
    for a in range(5):
        own(a).start()
    for p in range(pieces):
        own_weight(p).start()

    for s in (1, 2):
        for p in range(pieces):
            take_chain(s, p)
    for p in range(pieces):
        take_y(1, p)
    wait_inputs((0, 1, 2, 3, 4))

    slot_at = lax.broadcasted_iota(jnp.int32, (1, MCAP), 1)
    parts = [jnp.zeros((1, n * rows), jnp.float32)]
    for s in range(count_ref.shape[1]):
        factor = jnp.full((1, MCAP), factor_ref[0, s], jnp.int32).astype(jnp.float32)
        parts.append(jnp.where(slot_at < count_ref[0, s], jnp.log(factor) * LOG2E,
                               jnp.float32(-1.0e9)))
    bias_ref[...] = jnp.concatenate(parts, 1)

    keys = kbuf[...].reshape(2 * n * rows, width)
    vals = vbuf[...].reshape(2 * n * rows, width)
    head = z * 2 + c

    def lanes(h):
        return pl.ds(pl.multiple_of(h * width, width), width)

    def returning(level, xr, core):
        owner = level * plane + xr * 2 + core
        return pltpu.make_async_remote_copy(
            src_ref=att.at[owner], dst_ref=cols.at[lax.rem(xr + x, 2), :, lanes(head)],
            send_sem=ret_send.at[owner], recv_sem=ret_recv.at[lax.rem(xr + x, 2), head],
            device_id={"seq": level * plane + x * 2 + core}, device_id_type=mesh_id)

    def attend(j):
        level = lax.rem(z + nz // 2 + j, nz)
        queries = qbuf[pl.ds(level * plane, plane)].reshape(plane * rows, width)
        score = lax.dot_general(queries, keys, (((1,), (1,)), ((), ())),
                                preferred_element_type=jnp.float32)
        score = score * scale2 + bias_ref[...]
        top = jnp.max(score, axis=1, keepdims=True)
        prob = jnp.exp2(score - top)
        total = jnp.sum(prob, axis=1, keepdims=True)
        mixed = jnp.dot(prob.astype(jnp.bfloat16), vals, preferred_element_type=jnp.float32)
        att[pl.ds(level * plane, plane)] = (
            (mixed / total).astype(jnp.bfloat16).reshape(plane, rows, width))
        for core in range(2):
            for xr in range(2):
                @pl.when((level != z) | (core != c))
                def _():
                    returning(level, xr, core).start()

    for j in range(nz):
        attend(j)
        if j == 1:
            take_chain(3, 0)
            take_y(2, 0)
        if j == 2:
            for p in range(1, pieces):
                take_chain(3, p)

    for xr in range(2):
        keep = pltpu.make_async_copy(
            att.at[z * plane + xr * 2 + c], cols.at[lax.rem(xr + x, 2), :, lanes(head)],
            own_sem.at[xr])
        keep.start()
        keep.wait()

    take_y(3, 0)
    for p in range(1, pieces):
        take_y(2, p)

    def last_core(p):
        def act(d, level):
            for half in range(2):
                over_core(level, half, 1 - c, p).wait_recv()
        for s in range(1, nz):
            each_level(s, act)
        own_weight(p).wait()
        to_sibling(1 - c, p).wait_recv()

    @pl.loop(0, 2 * nz)
    def _(h):
        for slot in range(2):
            @pl.when(h != head)
            def _():
                pltpu.make_async_remote_copy(
                    src_ref=att.at[0], dst_ref=cols.at[slot, :, lanes(h)],
                    send_sem=ret_send.at[0], recv_sem=ret_recv.at[slot, h],
                    device_id={"seq": sibling}, device_id_type=mesh_id).wait_recv()

    tiles, tile = landed.shape[0], landed.shape[2]
    left = jnp.concatenate([cols[0], cols[1]], 0)

    def crossing(t):
        return pltpu.make_async_remote_copy(
            src_ref=theirs.at[t], dst_ref=landed.at[t],
            send_sem=out_send.at[t], recv_sem=out_recv.at[t],
            device_id={"seq": across}, device_id_type=mesh_id)

    for t in range(tiles):
        p, first = t * tile // span, t * tile % span
        if first == 0:
            if p:
                take_y(3, p)
            last_core(p)
        right = wbuf[p, :, :, :, first:first + tile].reshape(2 * nz * width, tile)
        mixed = jnp.dot(left, right, preferred_element_type=jnp.float32)
        theirs[t] = mixed[rows:].astype(jnp.bfloat16)
        crossing(t).start()
        mine[t] = mixed[:rows]
    for t in range(tiles):
        crossing(t).wait_recv()
        out_ref[:, t * tile:(t + 1) * tile] = (
            mine[t] + landed[t].astype(jnp.float32)).astype(out_ref.dtype)

    @pl.loop(1, n)
    def _(step):
        peer = lax.rem(me + step, n)
        for a in range(5):
            moving(a, peer, me).wait_send()

    @pl.loop(0, nz)
    def _(level):
        for core in range(2):
            for xr in range(2):
                @pl.when((level != z) | (core != c))
                def _():
                    returning(level, xr, core).wait_send()

    for i, d in enumerate((1, -1)):
        @pl.when((z + d >= 0) & (z + d < nz))
        def _():
            for p in range(pieces):
                along_own(i, d, p).wait_send()

    def sent_on(d, level):
        for p in range(pieces):
            over_y(level, g, p).wait_send()
            over_core(level, 0, c, p).wait_send()
            over_core(level, 1, c, p).wait_send()

    def forwarded(d, level):
        for p in range(pieces):
            along(d, level, p).wait_send()

    for s in range(1, nz - 1):
        each_forward(s, forwarded)
    for s in range(1, nz):
        each_level(s, sent_on)
    for p in range(pieces):
        to_sibling(c, p).wait_send()
    for t in range(tiles):
        crossing(t).wait_send()


def per_device_direct(query, key, value, mem_key, mem_value, mem_count, mem_factor, out_weight):
    _, heads, rows, width = query.shape
    n = heads
    depth, feat = out_weight.shape
    nz = n // 4
    tile = 512
    bf16 = query.dtype
    dma = pltpu.SemaphoreType.DMA
    result = pl.pallas_call(
        functools.partial(block_kernel, n, nz, width ** (-0.5) * LOG2E),
        out_shape=jax.ShapeDtypeStruct((rows, feat), bf16),
        in_specs=[pl.BlockSpec(memory_space=pltpu.HBM)] * 6 + [pl.BlockSpec(memory_space=pltpu.SMEM)] * 2,
        out_specs=pl.BlockSpec(memory_space=pltpu.VMEM),
        scratch_shapes=[
            pltpu.VMEM((n, rows, width), bf16),
            pltpu.VMEM((2 * n, rows, width), bf16),
            pltpu.VMEM((2 * n, rows, width), bf16),
            pltpu.VMEM((n, rows, width), bf16),
            pltpu.VMEM((PIECES, 2 * nz, 2, depth // 2, feat // PIECES), bf16),
            pltpu.VMEM((2, rows, 2 * nz * width), bf16),
            pltpu.VMEM((feat // tile, rows, tile), jnp.float32),
            pltpu.VMEM((feat // tile, rows, tile), bf16),
            pltpu.VMEM((feat // tile, rows, tile), bf16),
            pltpu.VMEM((1, 2 * n * rows), jnp.float32),
            dma((5, n)), dma((5, n)), dma((5,)), dma((PIECES,)), dma((PIECES,)), dma((PIECES,)),
            dma((nz + 2, PIECES)), dma((nz, PIECES)), dma((nz, PIECES)), dma((nz, PIECES)),
            dma((nz, 2, PIECES)), dma((nz, 2, PIECES)), dma((n,)), dma((2, 2 * nz)),
            dma((feat // tile,)), dma((feat // tile,)),
        ],
        compiler_params=pltpu.CompilerParams(
            collective_id=0, has_side_effects=True, vmem_limit_bytes=62 << 20),
    )(query, key, value, mem_key, mem_value, out_weight.reshape(2, depth // 2, feat),
      mem_count, mem_factor)
    return result[None]


def solution(mesh):
    in_specs = (
        P("grp", None, "seq", None),
        P("grp", None, "seq", None),
        P("grp", None, "seq", None),
        P("grp", None, "seq", None),
        P("grp", None, "seq", None),
        P("grp", None),
        P("grp", None),
        P("seq", None),
    )
    out_specs = P("grp", "seq", None)

    def program(query, key, value, mem_key, mem_value, mem_count, mem_factor, out_weight):
        direct = (
            query.shape[0] == mesh.shape["grp"]
            and query.shape[1] == mesh.shape["seq"]
            and mesh.shape["grp"] == 2
            and query.shape[1] == 16
            and out_weight.shape[0] == query.shape[1] * query.shape[3]
            and query.shape[3] == 128
            and out_weight.shape[1] % (512 * PIECES) == 0
            and mem_key.shape[2] == mem_count.shape[1] * MCAP
            and query.shape[2] == mem_key.shape[2]
            and (query.shape[2] // mesh.shape["seq"]) % 16 == 0
        )
        body = per_device_direct if direct else per_device
        return jax.shard_map(
            body, mesh=mesh, in_specs=in_specs, out_specs=out_specs, check_vma=False
        )(query, key, value, mem_key, mem_value, mem_count, mem_factor, out_weight)

    return program
```
